256 devices in a mesh: replica: 4 (over z_hi, core), fsdp: 64 (over z_lo, x, y).
Axes of the slice: x: 4, y: 4, z: 8 (z_hi: 2, z_lo: 4; z = z_hi * 4 + z_lo), core: 2. Of those that a mesh axis runs over, the one named last changes fastest.
Arguments:
- tokens: bfloat16 [65536, 2048], P(('replica', 'fsdp')), may hold values from -6 to 6
- inner_q: bfloat16 [4, 2048, 2048], P('replica', 'fsdp')
- inner_k: bfloat16 [4, 2048, 512], P('replica', 'fsdp')
- inner_v: bfloat16 [4, 2048, 512], P('replica', 'fsdp')
- outer_q: float32 [2048, 2048], P('fsdp')
- outer_k: float32 [2048, 512], P('fsdp')
- outer_v: float32 [2048, 512], P('fsdp')
- moment_q: float32 [2048, 2048], P('fsdp', 'replica'), may hold values from -0.09375 to 0.09375
- moment_k: float32 [2048, 512], P('fsdp', 'replica'), may hold values from -0.09375 to 0.09375
- value_momentum: float32 [2048, 512], P('fsdp', 'replica'), may hold values from -0.09375 to 0.09375
Outputs:
- projected: bfloat16 [65536, 3072], P(('replica', 'fsdp'))
- updated_outer_query: float32 [2048, 2048], P('fsdp')
- updated_outer_key: float32 [2048, 512], P('fsdp')
- new_outer_v: float32 [2048, 512], P('fsdp')
- new_moment_q: float32 [2048, 2048], P('fsdp', 'replica')
- new_moment_k: float32 [2048, 512], P('fsdp', 'replica')
- new_moment_v: float32 [2048, 512], P('fsdp', 'replica')
The draws below stay inside these ranges and needn't reach their ends.
All inputs are finite; a program needn't handle non-finite values.
Results may differ from the reference program's by a relative error of at most 0.005.
Values may be sent and summed in bfloat16 or wider, within the bound.
A program may use at most 64 MiB of HBM per device.

```python
import jax
import jax.numpy as jnp

D = 2048
HQ = 32
KEY_VALUE_HEADS = 8
HEAD_SIZE = 64
QCOLS = 2048
KVCOLS = 512
TOKENS = 65536
N_REPLICA = 4


def unit_noise(key, shape):
    return jnp.clip(jax.random.normal(key, shape, jnp.float32), -6.0, 6.0)


def outer_starting_weight(key, salt, columns):
    return unit_noise(jax.random.fold_in(key, salt), (D, columns)) / jnp.sqrt(jnp.float32(D))


def inner_weights_from(key, salt, columns):
    base = outer_starting_weight(key, salt, columns)
    drift = unit_noise(jax.random.fold_in(key, salt + 100), (N_REPLICA, D, columns))
    return (base[None] + 0.3 * drift / jnp.sqrt(jnp.float32(D))).astype(jnp.bfloat16)


def draw_outer_q(key, part):
    return outer_starting_weight(key, 1, HQ * HEAD_SIZE)


def draw_outer_k(key, part):
    return outer_starting_weight(key, 2, KEY_VALUE_HEADS * HEAD_SIZE)


def draw_outer_v(key, part):
    return outer_starting_weight(key, 3, KEY_VALUE_HEADS * HEAD_SIZE)


def draw_inner_q(key, part):
    return inner_weights_from(key, 1, HQ * HEAD_SIZE)


def draw_inner_k(key, part):
    return inner_weights_from(key, 2, KEY_VALUE_HEADS * HEAD_SIZE)


def draw_inner_v(key, part):
    return inner_weights_from(key, 3, KEY_VALUE_HEADS * HEAD_SIZE)


def block_scale(rng, dims, shards, least, top_value):
    def one(dim, blocks):
        steps = jax.random.uniform(jax.random.fold_in(jax.random.fold_in(rng, 6), dim), (blocks,), jnp.float32, least / len(shards), top_value / len(shards))
        return jnp.repeat(jnp.exp(steps), dims[dim] // blocks).reshape((-1,) + (1,) * (len(dims) - dim - 1))

    level = one(*shards[0])
    for cut in shards[1:]:
        level = level * one(*cut)
    return level


def normal_values(key, shape, scale, bound, cuts=(), dtype=jnp.bfloat16):
    entries = jax.random.normal(key, shape, jnp.float32) * scale
    if len(cuts) > 0:
        entries = block_scale(key, shape, cuts, -0.22, 0.18) * entries
    return jnp.clip(entries, min=-bound, max=bound).astype(dtype)


def setup_inputs(seed: int = 0) -> dict:
    splits = jax.random.split(jax.random.key(seed), 11)
    return {
        "tokens": normal_values(splits[0], (TOKENS, D), 1.0, 6.0, ((0, 256),)),
        "inner_q": draw_inner_q(jax.random.fold_in(splits[10], 71), 0),
        "inner_k": draw_inner_k(jax.random.fold_in(splits[10], 71), 0),
        "inner_v": draw_inner_v(jax.random.fold_in(splits[10], 71), 0),
        "outer_q": draw_outer_q(jax.random.fold_in(splits[10], 71), 0),
        "outer_k": draw_outer_k(jax.random.fold_in(splits[10], 71), 0),
        "outer_v": draw_outer_v(jax.random.fold_in(splits[10], 71), 0),
        "moment_q": normal_values(splits[7], (D, QCOLS), (0.3 / D ** 0.5), 0.09375, ((0, 64), (1, 4)), jnp.float32),
        "moment_k": normal_values(splits[8], (D, KVCOLS), (0.3 / D ** 0.5), 0.09375, ((0, 64), (1, 4)), jnp.float32),
        "value_momentum": normal_values(splits[9], (D, KVCOLS), (0.3 / D ** 0.5), 0.09375, ((0, 64), (1, 4)), jnp.float32),
    }


def outer_step(inner, outer, outer_momentum):
    pseudo = jnp.sum(outer[None] - inner.astype(jnp.float32), axis=0) / N_REPLICA
    new_moment = 0.9 * outer_momentum + pseudo
    new_outer = outer - 0.7 * (pseudo + 0.9 * new_moment)
    return new_outer, new_moment


def reference(tokens, inner_q, inner_k, inner_v, outer_q, outer_k, outer_v, moment_q, moment_k, value_momentum):
    updated_outer_query, new_moment_q = outer_step(inner_q, outer_q, moment_q)
    updated_outer_key, new_moment_k = outer_step(inner_k, outer_k, moment_k)
    new_outer_v, new_moment_v = outer_step(inner_v, outer_v, value_momentum)
    fresh = jnp.concatenate([updated_outer_query, updated_outer_key, new_outer_v], axis=1).astype(jnp.bfloat16)
    projected = jnp.dot(tokens, fresh, preferred_element_type=jnp.float32).astype(jnp.bfloat16)
    return projected, updated_outer_query, updated_outer_key, new_outer_v, new_moment_q, new_moment_k, new_moment_v
```

```python
import functools
import heapq

import jax
import jax.numpy as jnp
from jax import lax
from jax.experimental import pallas as pl
from jax.experimental.pallas import tpu as pltpu
from jax.sharding import PartitionSpec as P

LEARN_RATE = 0.7
MOMENTUM_BETA = 0.9
MESH = pl.DeviceIdType.MESH

NX, NY, NZ = 4, 4, 8
SIZE = {"x": NX, "y": NY, "z": NZ}
ROWS = 32
WIDTH = 256
ORDERS = (("x", "y", "z"), ("z", "y", "x"), ("z", "x", "y"))


def subs_of(colour, phase):
    if phase == 0:
        return (None,)
    if colour == 0:
        return (None,) if phase == 1 else tuple((d, None) for d in (0, 3, 1, 2))
    if phase == 1:
        return (0, 1)
    return tuple((d, k) for d in (0, 3, 1, 2) for k in (0, 1))


def reach(colour, phase, sub):
    n = SIZE[ORDERS[colour][phase]]
    subs = subs_of(colour, phase)
    odd = subs.index(sub) % 2 if len(subs) > 1 else (colour + phase) % 2
    return (n // 2, n - 1 - n // 2) if odd == 0 else (n - 1 - n // 2, n // 2)


def all_messages():
    out = []
    for colour in range(3):
        for phase in range(3):
            for sub in subs_of(colour, phase):
                plus, minus = reach(colour, phase, sub)
                out += [(colour, phase, sub, 1, s) for s in range(1, plus + 1)]
                out += [(colour, phase, sub, -1, s) for s in range(1, minus + 1)]
    return out


MESSAGES = all_messages()
INDEX = {m: i for i, m in enumerate(MESSAGES)}


class Flow:
    def __init__(self, send):
        self.send = send
        self.first = [0, 0, 0]

    def begin(self, colour, phase, sub):
        plus, minus = reach(colour, phase, sub)
        for direction, hops in ((1, plus), (-1, minus)):
            if hops >= 1:
                self.send((colour, phase, sub, direction, 1))

    def received(self, message):
        colour, phase, sub, direction, step = message
        plus, minus = reach(colour, phase, sub)
        if step < (plus if direction == 1 else minus):
            self.send((colour, phase, sub, direction, step + 1))
        if phase == 0:
            self.first[colour] += 1
            if self.first[colour] == SIZE[ORDERS[colour][0]] - 1:
                for k in subs_of(colour, 1):
                    self.begin(colour, 1, k)
                for k in subs_of(colour, 1):
                    self.begin(colour, 2, (0, k))
        elif phase == 1:
            offset = (-direction * step) % SIZE[ORDERS[colour][1]]
            self.begin(colour, 2, (offset, sub))


def plan(starts):
    free, heap = {}, []
    now = [0.0]

    def send(message):
        colour, phase, sub, direction, step = message
        size = 16384 if phase == 0 else 65536
        link = (ORDERS[colour][phase], direction)
        begin = max(now[0], free.get(link, 0.0))
        free[link] = begin + size / 46e3
        heapq.heappush(heap, (free[link] + 1.7, INDEX[message]))

    flow = Flow(send)
    order = []
    for colour, start in enumerate(starts):
        heapq.heappush(heap, (start, -1 - colour))
    while heap:
        now[0], which = heapq.heappop(heap)
        order.append(which)
        if which < 0:
            flow.begin(-1 - which, 0, None)
        else:
            flow.received(MESSAGES[which])
    return order, now[0]


PLAN, MODEL_TIME = plan((3.0, 0.0, 1.5))


def kernel(
    tok, iq, ik, iv, oq, ok, ov, mq, mk, mv,
    proj, uq, uk, uv, nq, nk, nv,
    buf, tok2, ri, fr, pout,
    rep_sem, ring_sem, tok_sem, fr_sem, out_sem, rep_send, ring_send, fr_send, out_send, tok_send, tok_local,
):
    r, f = lax.axis_index("replica"), lax.axis_index("fsdp")
    core, zh = r % 2, r // 2
    zl, x, y = f // 16, (f // 4) % 4, f % 4
    z = zh * 4 + zl
    at = {"x": x, "y": y, "z": z}

    def dev(xx, yy, zz):
        return {"replica": (zz // 4) * 2 + core, "fsdp": ((zz % 4) * 4 + xx) * 4 + yy}

    def neighbour(axis, direction):
        moved = dict(at)
        moved[axis] = (at[axis] + direction + SIZE[axis]) % SIZE[axis]
        return dev(moved["x"], moved["y"], moved["z"])

    peer_index = (zh * 2 + (1 - core), (1 - zh) * 2 + core, (1 - zh) * 2 + (1 - core))
    peers = tuple({"replica": p, "fsdp": f} for p in peer_index)
    neighbours = {(a, d): neighbour(a, d) for a in ("x", "y", "z") for d in (1, -1)}

    barrier = pltpu.get_barrier_semaphore()
    for target in peers + tuple(neighbours.values()):
        pl.semaphore_signal(barrier, inc=1, device_id=target, device_id_type=MESH)
    own_tokens = pltpu.make_async_copy(tok, tok2.at[0], tok_local)
    own_tokens.start()
    pl.semaphore_wait(barrier, 9)

    def remote(src, dst, send_sem, recv_sem, target):
        return pltpu.make_async_remote_copy(
            src_ref=src, dst_ref=dst, send_sem=send_sem, recv_sem=recv_sem, device_id=target, device_id_type=MESH
        )

    def col(index, width, extra=0):
        return pl.ds(pl.multiple_of(index * width + extra, 128), WIDTH if width == 512 else 128)

    def replica_copies(colour, d):
        p = peer_index[d]
        if colour < 2:
            pairs = ((iq.at[:, col(p, 512, colour * WIDTH)], ri.at[d, colour]),)
        else:
            pairs = (
                (ik.at[:, col(p, 128)], ri.at[d, 2, :, 0:128]),
                (iv.at[:, col(p, 128)], ri.at[d, 2, :, 128:256]),
            )
        return [
            remote(src, dst, rep_send.at[d, colour + i], rep_sem.at[d, colour + i], peers[d])
            for i, (src, dst) in enumerate(pairs)
        ]

    copies = {}
    for colour in (1, 2, 0):
        for d in (1, 2, 0):
            copies[colour, d] = replica_copies(colour, d)
            for c in copies[colour, d]:
                c.start()
    swap = remote(tok, tok2.at[1], tok_send, tok_sem, peers[0])
    swap.start()

    def update(colour):
        for d in range(3):
            for c in copies[colour, d]:
                c.wait_recv()
        if colour < 2:
            outer = oq[:, col(r, 512, colour * WIDTH)]
            inner = iq[:, col(r, 512, colour * WIDTH)]
            moment = mq[:, colour * WIDTH:(colour + 1) * WIDTH]
        else:
            outer = jnp.concatenate([ok[:, col(r, 128)], ov[:, col(r, 128)]], axis=1)
            inner = jnp.concatenate([ik[:, col(r, 128)], iv[:, col(r, 128)]], axis=1)
            moment = jnp.concatenate([mk[...], mv[...]], axis=1)
        total = outer - inner.astype(jnp.float32)
        for d in range(3):
            total += outer - ri[d, colour].astype(jnp.float32)
        pseudo = total * 0.25
        new_moment = MOMENTUM_BETA * moment + pseudo
        new_outer = outer - LEARN_RATE * (pseudo + MOMENTUM_BETA * new_moment)
        buf[colour, z, x, y] = new_outer.astype(jnp.bfloat16)
        if colour < 2:
            nq[:, colour * WIDTH:(colour + 1) * WIDTH] = new_moment
        else:
            nk[...] = new_moment[:, :128]
            nv[...] = new_moment[:, 128:]

    def block(colour, phase, sub, offset):
        axis = ORDERS[colour][phase]
        pos = dict(at)
        if phase == 2:
            second = ORDERS[colour][1]
            pos[second] = (at[second] + sub[0]) % SIZE[second]
            sub = sub[1]
        pos[axis] = (at[axis] + offset + SIZE[axis]) % SIZE[axis]
        if phase == 0:
            return buf.at[colour, pos["z"], pos["x"], pos["y"]]
        if colour == 0:
            return buf.at[0, pos["z"], :, pos["y"]]
        return buf.at[colour, pl.ds(sub * 4, 4), pos["x"], pos["y"]]

    def ring_copy(message):
        colour, phase, sub, direction, step = message
        src = block(colour, phase, sub, -direction * (step - 1))
        return remote(src, src, ring_send, ring_sem.at[INDEX[message]], neighbours[ORDERS[colour][phase], direction])

    def wait_ring(message):
        colour, phase, sub, direction, step = message
        dst = block(colour, phase, sub, -direction * step)
        remote(dst, dst, ring_send, ring_sem.at[INDEX[message]], neighbours[ORDERS[colour][phase], direction]).wait_recv()

    flow = Flow(lambda message: ring_copy(message).start())
    partner_copies = []
    for which in PLAN:
        if which < 0:
            colour = -1 - which
            update(colour)
            flow.begin(colour, 0, None)
            c = remote(buf.at[colour, z, x, y], fr.at[0, colour], fr_send.at[0, colour], fr_sem.at[0, colour], peers[0])
            c.start()
            partner_copies.append(c)
        else:
            wait_ring(MESSAGES[which])
            flow.received(MESSAGES[which])

    z4 = (z + 4) % 8
    for colour in range(3):
        c = remote(buf.at[colour, z4, x, y], fr.at[1, colour], fr_send.at[1, colour], fr_sem.at[1, colour], peers[0])
        c.start()
        partner_copies.append(c)

    own_tokens.wait()
    swap.wait()

    out_copies = []

    def send_out(i):
        colour, h = i // 2, i % 2
        rr = 2 * h + core
        if colour < 2:
            pairs = ((pout.at[i], proj.at[:, col(rr, 512, colour * WIDTH)]),)
        else:
            pairs = (
                (pout.at[i, :, 0:128], proj.at[:, col(rr, 128, 2048)]),
                (pout.at[i, :, 128:256], proj.at[:, col(rr, 128, 2560)]),
            )
        for j, (src, dst) in enumerate(pairs):
            c = remote(src, dst, out_send.at[i, j], out_sem.at[i, j], peers[0])
            c.start()
            out_copies.append(c)

    for i in range(6):
        colour, h = i // 2, i % 2
        rr = 2 * h + core
        w = buf[colour, h * 4:(h + 1) * 4].reshape(2048, WIDTH)
        acc = jnp.dot(tok2[...].reshape(512, 2048), w, preferred_element_type=jnp.float32).astype(jnp.bfloat16)
        pout[i] = acc[256:]
        if colour < 2:
            proj[:, col(rr, 512, colour * WIDTH)] = acc[:256]
        else:
            proj[:, col(rr, 128, 2048)] = acc[:256, :128]
            proj[:, col(rr, 128, 2560)] = acc[:256, 128:]
        if i >= 1:
            send_out(i - 1)
    send_out(5)

    for c in partner_copies:
        c.wait()
    for source, owner in (
        (lambda c: buf[c, z, x, y], r),
        (lambda c: buf[c, z4, x, y], peer_index[1]),
        (lambda c: fr[0, c], peer_index[0]),
        (lambda c: fr[1, c], peer_index[2]),
    ):
        for colour in range(2):
            uq[:, col(owner, 512, colour * WIDTH)] = source(colour).astype(jnp.float32)
        both = source(2).astype(jnp.float32)
        uk[:, col(owner, 128)] = both[:, :128]
        uv[:, col(owner, 128)] = both[:, 128:]

    for c in out_copies:
        c.wait()
    for colour in range(3):
        for d in range(3):
            for c in copies[colour, d]:
                c.wait_send()
    for colour in range(3):
        done = buf.at[colour].reshape(128, ROWS, WIDTH).at[pl.ds(0, 127)]
        pltpu.make_async_copy(done, done, ring_send).wait()


def per_device(
    tokens, inner_q, inner_k, inner_v, outer_q, outer_k, outer_v, moment_q, moment_k, value_momentum
):
    f32, bf16 = jnp.float32, jnp.bfloat16
    vmem = pl.BlockSpec(memory_space=pltpu.VMEM)
    out = pl.pallas_call(
        kernel,
        out_shape=(
            jax.ShapeDtypeStruct((256, 3072), bf16),
            jax.ShapeDtypeStruct((ROWS, 2048), f32),
            jax.ShapeDtypeStruct((ROWS, 512), f32),
            jax.ShapeDtypeStruct((ROWS, 512), f32),
            jax.ShapeDtypeStruct((ROWS, 512), f32),
            jax.ShapeDtypeStruct((ROWS, 128), f32),
            jax.ShapeDtypeStruct((ROWS, 128), f32),
        ),
        in_specs=[pl.BlockSpec(memory_space=pl.ANY)] + [vmem] * 9,
        out_specs=(vmem,) * 7,
        scratch_shapes=[
            pltpu.VMEM((3, NZ, NX, NY, ROWS, WIDTH), bf16),
            pltpu.VMEM((2, 256, 2048), bf16),
            pltpu.VMEM((3, 3, ROWS, WIDTH), bf16),
            pltpu.VMEM((2, 3, ROWS, WIDTH), bf16),
            pltpu.VMEM((6, 256, WIDTH), bf16),
            pltpu.SemaphoreType.DMA((3, 4)),
            pltpu.SemaphoreType.DMA((len(MESSAGES),)),
            pltpu.SemaphoreType.DMA,
            pltpu.SemaphoreType.DMA((2, 3)),
            pltpu.SemaphoreType.DMA((6, 2)),
            pltpu.SemaphoreType.DMA((3, 4)),
            pltpu.SemaphoreType.DMA,
            pltpu.SemaphoreType.DMA((2, 3)),
            pltpu.SemaphoreType.DMA((6, 2)),
            pltpu.SemaphoreType.DMA,
            pltpu.SemaphoreType.DMA,
        ],
        compiler_params=pltpu.CompilerParams(
            collective_id=0, has_side_effects=True, vmem_limit_bytes=48 * 1024 * 1024
        ),
        name="outer_step_gather_project",
    )(tokens, inner_q[0], inner_k[0], inner_v[0], outer_q, outer_k, outer_v, moment_q, moment_k, value_momentum)
    return tuple(out)


def solution(mesh):
    placed = (
        P(("replica", "fsdp"), None),
        P("replica", "fsdp", None),
        P("replica", "fsdp", None),
        P("replica", "fsdp", None),
        P("fsdp", None),
        P("fsdp", None),
        P("fsdp", None),
        P("fsdp", "replica"),
        P("fsdp", "replica"),
        P("fsdp", "replica"),
    )
    return jax.shard_map(
        per_device,
        mesh=mesh,
        in_specs=placed,
        out_specs=(
            P(("replica", "fsdp"), None),
            P("fsdp", None),
            P("fsdp", None),
            P("fsdp", None),
            P("fsdp", "replica"),
            P("fsdp", "replica"),
            P("fsdp", "replica"),
        ),
        check_vma=False,
    )
```

```python
import functools
import heapq

import jax
import jax.numpy as jnp
from jax import lax
from jax.experimental import pallas as pl
from jax.experimental.pallas import tpu as pltpu
from jax.sharding import PartitionSpec as P

LEARN_RATE = 0.7
MOMENTUM_BETA = 0.9
MESH = pl.DeviceIdType.MESH

NX, NY, NZ = 4, 4, 8
SIZE = {"x": NX, "y": NY, "z": NZ}
ROWS = 32
WIDTH = 256
ORDERS = (("x", "y", "z"), ("z", "y", "x"), ("z", "x", "y"))


def subs_of(colour, phase):
    if phase == 0:
        return (None,)
    if colour == 0:
        return (None,) if phase == 1 else tuple((d, None) for d in (0, 3, 1, 2))
    if phase == 1:
        return (0, 1)
    return tuple((d, k) for d in (0, 3, 1, 2) for k in (0, 1))


def reach(colour, phase, sub):
    n = SIZE[ORDERS[colour][phase]]
    subs = subs_of(colour, phase)
    odd = subs.index(sub) % 2 if len(subs) > 1 else (colour + phase) % 2
    return (n // 2, n - 1 - n // 2) if odd == 0 else (n - 1 - n // 2, n // 2)


def all_messages():
    out = []
    for colour in range(3):
        for phase in range(3):
            for sub in subs_of(colour, phase):
                plus, minus = reach(colour, phase, sub)
                out += [(colour, phase, sub, 1, s) for s in range(1, plus + 1)]
                out += [(colour, phase, sub, -1, s) for s in range(1, minus + 1)]
    return out


MESSAGES = all_messages()
INDEX = {m: i for i, m in enumerate(MESSAGES)}


class Flow:
    def __init__(self, send):
        self.send = send
        self.first = [0, 0, 0]

    def begin(self, colour, phase, sub):
        plus, minus = reach(colour, phase, sub)
        for direction, hops in ((1, plus), (-1, minus)):
            if hops >= 1:
                self.send((colour, phase, sub, direction, 1))

    def received(self, message):
        colour, phase, sub, direction, step = message
        plus, minus = reach(colour, phase, sub)
        if step < (plus if direction == 1 else minus):
            self.send((colour, phase, sub, direction, step + 1))
        if phase == 0:
            self.first[colour] += 1
            if self.first[colour] == SIZE[ORDERS[colour][0]] - 1:
                for k in subs_of(colour, 1):
                    self.begin(colour, 1, k)
                for k in subs_of(colour, 1):
                    self.begin(colour, 2, (0, k))
        elif phase == 1:
            offset = (-direction * step) % SIZE[ORDERS[colour][1]]
            self.begin(colour, 2, (offset, sub))


def plan(starts):
    free, heap = {}, []
    now = [0.0]

    def send(message):
        colour, phase, sub, direction, step = message
        size = 16384 if phase == 0 else 65536
        link = (ORDERS[colour][phase], direction)
        begin = max(now[0], free.get(link, 0.0))
        free[link] = begin + size / 46e3
        heapq.heappush(heap, (free[link] + 1.7, INDEX[message]))

    flow = Flow(send)
    order = []
    for colour, start in enumerate(starts):
        heapq.heappush(heap, (start, -1 - colour))
    while heap:
        now[0], which = heapq.heappop(heap)
        order.append(which)
        if which < 0:
            flow.begin(-1 - which, 0, None)
        else:
            flow.received(MESSAGES[which])
    return order, now[0]


PLAN, MODEL_TIME = plan((3.0, 0.0, 1.5))


def kernel(
    tok, iq_hbm, ik_hbm, iv_hbm, oq_hbm, ok_hbm, ov_hbm, mq_hbm, mk_hbm, mv_hbm,
    proj, uq, uk, uv, nq, nk, nv,
    iq, ik, iv, oq, ok, ov, mq, mk, mv, in_sem,
    buf, tok2, ri, fr, pout,
    rep_sem, ring_sem, tok_sem, fr_sem, out_sem, rep_send, ring_send, fr_send, out_send, tok_send, tok_local,
):
    r, f = lax.axis_index("replica"), lax.axis_index("fsdp")
    core, zh = r % 2, r // 2
    zl, x, y = f // 16, (f // 4) % 4, f % 4
    z = zh * 4 + zl
    at = {"x": x, "y": y, "z": z}

    def dev(xx, yy, zz):
        return {"replica": (zz // 4) * 2 + core, "fsdp": ((zz % 4) * 4 + xx) * 4 + yy}

    def neighbour(axis, direction):
        moved = dict(at)
        moved[axis] = (at[axis] + direction + SIZE[axis]) % SIZE[axis]
        return dev(moved["x"], moved["y"], moved["z"])

    peer_index = (zh * 2 + (1 - core), (1 - zh) * 2 + core, (1 - zh) * 2 + (1 - core))
    peers = tuple({"replica": p, "fsdp": f} for p in peer_index)
    neighbours = {(a, d): neighbour(a, d) for a in ("x", "y", "z") for d in (1, -1)}

    barrier = pltpu.get_barrier_semaphore()
    for target in peers + tuple(neighbours.values()):
        pl.semaphore_signal(barrier, inc=1, device_id=target, device_id_type=MESH)
    fetches = [
        pltpu.make_async_copy(src, dst, in_sem.at[i])
        for i, (src, dst) in enumerate(
            zip(
                (iq_hbm, ik_hbm, iv_hbm, oq_hbm, ok_hbm, ov_hbm, mq_hbm, mk_hbm, mv_hbm),
                (iq, ik, iv, oq, ok, ov, mq, mk, mv),
            )
        )
    ]
    for c in fetches:
        c.start()
    own_tokens = pltpu.make_async_copy(tok, tok2.at[0], tok_local)
    own_tokens.start()
    for c in fetches:
        c.wait()
    pl.semaphore_wait(barrier, 9)

    def remote(src, dst, send_sem, recv_sem, target):
        return pltpu.make_async_remote_copy(
            src_ref=src, dst_ref=dst, send_sem=send_sem, recv_sem=recv_sem, device_id=target, device_id_type=MESH
        )

    def col(index, width, extra=0):
        return pl.ds(pl.multiple_of(index * width + extra, 128), WIDTH if width == 512 else 128)

    def replica_copies(colour, d):
        p = peer_index[d]
        if colour < 2:
            pairs = ((iq.at[:, col(p, 512, colour * WIDTH)], ri.at[d, colour]),)
        else:
            pairs = (
                (ik.at[:, col(p, 128)], ri.at[d, 2, :, 0:128]),
                (iv.at[:, col(p, 128)], ri.at[d, 2, :, 128:256]),
            )
        return [
            remote(src, dst, rep_send.at[d, colour + i], rep_sem.at[d, colour + i], peers[d])
            for i, (src, dst) in enumerate(pairs)
        ]

    copies = {}
    for colour in (1, 2, 0):
        for d in (1, 2, 0):
            copies[colour, d] = replica_copies(colour, d)
            for c in copies[colour, d]:
                c.start()
    swap = remote(tok, tok2.at[1], tok_send, tok_sem, peers[0])
    swap.start()

    def update(colour):
        for d in range(3):
            for c in copies[colour, d]:
                c.wait_recv()
        if colour < 2:
            outer = oq[:, col(r, 512, colour * WIDTH)]
            inner = iq[:, col(r, 512, colour * WIDTH)]
            moment = mq[:, colour * WIDTH:(colour + 1) * WIDTH]
        else:
            outer = jnp.concatenate([ok[:, col(r, 128)], ov[:, col(r, 128)]], axis=1)
            inner = jnp.concatenate([ik[:, col(r, 128)], iv[:, col(r, 128)]], axis=1)
            moment = jnp.concatenate([mk[...], mv[...]], axis=1)
        total = outer - inner.astype(jnp.float32)
        for d in range(3):
            total += outer - ri[d, colour].astype(jnp.float32)
        pseudo = total * 0.25
        new_moment = MOMENTUM_BETA * moment + pseudo
        new_outer = outer - LEARN_RATE * (pseudo + MOMENTUM_BETA * new_moment)
        buf[colour, z, x, y] = new_outer.astype(jnp.bfloat16)
        if colour < 2:
            nq[:, colour * WIDTH:(colour + 1) * WIDTH] = new_moment
        else:
            nk[...] = new_moment[:, :128]
            nv[...] = new_moment[:, 128:]

    def block(colour, phase, sub, offset):
        axis = ORDERS[colour][phase]
        pos = dict(at)
        if phase == 2:
            second = ORDERS[colour][1]
            pos[second] = (at[second] + sub[0]) % SIZE[second]
            sub = sub[1]
        pos[axis] = (at[axis] + offset + SIZE[axis]) % SIZE[axis]
        if phase == 0:
            return buf.at[colour, pos["z"], pos["x"], pos["y"]]
        if colour == 0:
            return buf.at[0, pos["z"], :, pos["y"]]
        return buf.at[colour, pl.ds(sub * 4, 4), pos["x"], pos["y"]]

    def ring_copy(message):
        colour, phase, sub, direction, step = message
        src = block(colour, phase, sub, -direction * (step - 1))
        return remote(src, src, ring_send, ring_sem.at[INDEX[message]], neighbours[ORDERS[colour][phase], direction])

    def wait_ring(message):
        colour, phase, sub, direction, step = message
        dst = block(colour, phase, sub, -direction * step)
        remote(dst, dst, ring_send, ring_sem.at[INDEX[message]], neighbours[ORDERS[colour][phase], direction]).wait_recv()

    flow = Flow(lambda message: ring_copy(message).start())
    partner_copies = []
    for which in PLAN:
        if which < 0:
            colour = -1 - which
            update(colour)
            flow.begin(colour, 0, None)
            c = remote(buf.at[colour, z, x, y], fr.at[0, colour], fr_send.at[0, colour], fr_sem.at[0, colour], peers[0])
            c.start()
            partner_copies.append(c)
        else:
            wait_ring(MESSAGES[which])
            flow.received(MESSAGES[which])

    z4 = (z + 4) % 8
    for colour in range(3):
        c = remote(buf.at[colour, z4, x, y], fr.at[1, colour], fr_send.at[1, colour], fr_sem.at[1, colour], peers[0])
        c.start()
        partner_copies.append(c)

    own_tokens.wait()
    swap.wait()

    out_copies = []

    def send_out(i):
        colour, h = i // 2, i % 2
        rr = 2 * h + core
        if colour < 2:
            pairs = ((pout.at[i], proj.at[:, col(rr, 512, colour * WIDTH)]),)
        else:
            pairs = (
                (pout.at[i, :, 0:128], proj.at[:, col(rr, 128, 2048)]),
                (pout.at[i, :, 128:256], proj.at[:, col(rr, 128, 2560)]),
            )
        for j, (src, dst) in enumerate(pairs):
            c = remote(src, dst, out_send.at[i, j], out_sem.at[i, j], peers[0])
            c.start()
            out_copies.append(c)

    for i in range(6):
        colour, h = i // 2, i % 2
        rr = 2 * h + core
        w = buf[colour, h * 4:(h + 1) * 4].reshape(2048, WIDTH)
        acc = jnp.dot(tok2[...].reshape(512, 2048), w, preferred_element_type=jnp.float32).astype(jnp.bfloat16)
        pout[i] = acc[256:]
        if colour < 2:
            proj[:, col(rr, 512, colour * WIDTH)] = acc[:256]
        else:
            proj[:, col(rr, 128, 2048)] = acc[:256, :128]
            proj[:, col(rr, 128, 2560)] = acc[:256, 128:]
        if i >= 1:
            send_out(i - 1)
    send_out(5)

    for c in partner_copies:
        c.wait()
    for source, owner in (
        (lambda c: buf[c, z, x, y], r),
        (lambda c: buf[c, z4, x, y], peer_index[1]),
        (lambda c: fr[0, c], peer_index[0]),
        (lambda c: fr[1, c], peer_index[2]),
    ):
        for colour in range(2):
            uq[:, col(owner, 512, colour * WIDTH)] = source(colour).astype(jnp.float32)
        both = source(2).astype(jnp.float32)
        uk[:, col(owner, 128)] = both[:, :128]
        uv[:, col(owner, 128)] = both[:, 128:]

    for c in out_copies:
        c.wait()
    for colour in range(3):
        for d in range(3):
            for c in copies[colour, d]:
                c.wait_send()
    for colour in range(3):
        done = buf.at[colour].reshape(128, ROWS, WIDTH).at[pl.ds(0, 127)]
        pltpu.make_async_copy(done, done, ring_send).wait()


def write_kernel(*refs):
    sources, targets, sem = refs[:7], refs[7:14], refs[14]
    copies = [pltpu.make_async_copy(src, dst, sem.at[i]) for i, (src, dst) in enumerate(zip(sources, targets))]
    for c in copies:
        c.start()
    for c in copies:
        c.wait()


def write_out(results):
    return pl.pallas_call(
        write_kernel,
        out_shape=tuple(jax.ShapeDtypeStruct(a.shape, a.dtype) for a in results),
        in_specs=[pl.BlockSpec(memory_space=pltpu.VMEM)] * 7,
        out_specs=(pl.BlockSpec(memory_space=pltpu.HBM),) * 7,
        scratch_shapes=[pltpu.SemaphoreType.DMA((7,))],
        compiler_params=pltpu.CompilerParams(vmem_limit_bytes=16 * 1024 * 1024),
        name="write_results",
    )(*results)


def per_device(
    tokens, inner_q, inner_k, inner_v, outer_q, outer_k, outer_v, moment_q, moment_k, value_momentum
):
    f32, bf16 = jnp.float32, jnp.bfloat16
    vmem = pl.BlockSpec(memory_space=pltpu.VMEM)
    out = pl.pallas_call(
        kernel,
        out_shape=(
            jax.ShapeDtypeStruct((256, 3072), bf16),
            jax.ShapeDtypeStruct((ROWS, 2048), f32),
            jax.ShapeDtypeStruct((ROWS, 512), f32),
            jax.ShapeDtypeStruct((ROWS, 512), f32),
            jax.ShapeDtypeStruct((ROWS, 512), f32),
            jax.ShapeDtypeStruct((ROWS, 128), f32),
            jax.ShapeDtypeStruct((ROWS, 128), f32),
        ),
        in_specs=[pl.BlockSpec(memory_space=pltpu.HBM)] * 10,
        out_specs=(vmem,) * 7,
        scratch_shapes=[
            pltpu.VMEM((ROWS, 2048), bf16),
            pltpu.VMEM((ROWS, 512), bf16),
            pltpu.VMEM((ROWS, 512), bf16),
            pltpu.VMEM((ROWS, 2048), f32),
            pltpu.VMEM((ROWS, 512), f32),
            pltpu.VMEM((ROWS, 512), f32),
            pltpu.VMEM((ROWS, 512), f32),
            pltpu.VMEM((ROWS, 128), f32),
            pltpu.VMEM((ROWS, 128), f32),
            pltpu.SemaphoreType.DMA((9,)),
            pltpu.VMEM((3, NZ, NX, NY, ROWS, WIDTH), bf16),
            pltpu.VMEM((2, 256, 2048), bf16),
            pltpu.VMEM((3, 3, ROWS, WIDTH), bf16),
            pltpu.VMEM((2, 3, ROWS, WIDTH), bf16),
            pltpu.VMEM((6, 256, WIDTH), bf16),
            pltpu.SemaphoreType.DMA((3, 4)),
            pltpu.SemaphoreType.DMA((len(MESSAGES),)),
            pltpu.SemaphoreType.DMA,
            pltpu.SemaphoreType.DMA((2, 3)),
            pltpu.SemaphoreType.DMA((6, 2)),
            pltpu.SemaphoreType.DMA((3, 4)),
            pltpu.SemaphoreType.DMA,
            pltpu.SemaphoreType.DMA((2, 3)),
            pltpu.SemaphoreType.DMA((6, 2)),
            pltpu.SemaphoreType.DMA,
            pltpu.SemaphoreType.DMA,
        ],
        compiler_params=pltpu.CompilerParams(
            collective_id=0, has_side_effects=True, vmem_limit_bytes=32 * 1024 * 1024
        ),
        name="outer_step_gather_project",
    )(*(
        pltpu.with_memory_space_constraint(a, pltpu.HBM)
        for a in (
            tokens, inner_q[0], inner_k[0], inner_v[0], outer_q, outer_k, outer_v, moment_q, moment_k, value_momentum
        )
    ))
    return tuple(write_out(out))


def solution(mesh):
    placed = (
        P(("replica", "fsdp"), None),
        P("replica", "fsdp", None),
        P("replica", "fsdp", None),
        P("replica", "fsdp", None),
        P("fsdp", None),
        P("fsdp", None),
        P("fsdp", None),
        P("fsdp", "replica"),
        P("fsdp", "replica"),
        P("fsdp", "replica"),
    )
    return jax.shard_map(
        per_device,
        mesh=mesh,
        in_specs=placed,
        out_specs=(
            P(("replica", "fsdp"), None),
            P("fsdp", None),
            P("fsdp", None),
            P("fsdp", None),
            P("fsdp", "replica"),
            P("fsdp", "replica"),
            P("fsdp", "replica"),
        ),
        check_vma=False,
    )
```

```python
import functools
import heapq

import jax
import jax.numpy as jnp
from jax import lax
from jax.experimental import pallas as pl
from jax.experimental.pallas import tpu as pltpu
from jax.sharding import PartitionSpec as P

LEARN_RATE = 0.7
MOMENTUM_BETA = 0.9
MESH = pl.DeviceIdType.MESH

NX, NY, NZ = 4, 4, 8
SIZE = {"x": NX, "y": NY, "z": NZ}
ROWS = 32
WIDTH = 256
ORDERS = (("x", "y", "z"), ("z", "y", "x"), ("z", "x", "y"))


def subs_of(colour, phase):
    if phase == 0:
        return (None,)
    if colour == 0:
        return (None,) if phase == 1 else tuple((d, None) for d in (0, 3, 1, 2))
    if phase == 1:
        return (0, 1)
    return tuple((d, k) for d in (0, 3, 1, 2) for k in (0, 1))


def reach(colour, phase, sub):
    n = SIZE[ORDERS[colour][phase]]
    subs = subs_of(colour, phase)
    odd = subs.index(sub) % 2 if len(subs) > 1 else (colour + phase) % 2
    return (n // 2, n - 1 - n // 2) if odd == 0 else (n - 1 - n // 2, n // 2)


def all_messages():
    out = []
    for colour in range(3):
        for phase in range(3):
            for sub in subs_of(colour, phase):
                plus, minus = reach(colour, phase, sub)
                out += [(colour, phase, sub, 1, s) for s in range(1, plus + 1)]
                out += [(colour, phase, sub, -1, s) for s in range(1, minus + 1)]
    return out


MESSAGES = all_messages()
INDEX = {m: i for i, m in enumerate(MESSAGES)}


class Flow:
    def __init__(self, send, ready):
        self.send, self.ready = send, ready
        self.first = [0, 0, 0]
        self.missing = {(0, o): 4 if o else 6 for o in range(8)}
        self.missing.update({(1, k): 22 for k in (0, 1)})
        self.missing.update({(2, d, k): 4 if d else 10 for d in range(4) for k in (0, 1)})

    def count(self, message):
        colour, phase, sub, direction, step = message
        offset = (-direction * step) % SIZE[ORDERS[colour][phase]]
        if colour == 0:
            pieces = ((0, offset if phase == 2 else 0),)
        elif colour == 1:
            pieces = ((1, 0), (1, 1)) if phase == 0 else ((1, sub if phase == 1 else sub[1]),)
        elif phase == 0:
            pieces = ((2, 0, 0), (2, 0, 1))
        else:
            pieces = ((2, offset, sub),) if phase == 1 else ((2,) + sub,)
        for piece in pieces:
            self.missing[piece] -= 1
            if self.missing[piece] == 0:
                self.ready(piece)

    def begin(self, colour, phase, sub):
        plus, minus = reach(colour, phase, sub)
        for direction, hops in ((1, plus), (-1, minus)):
            if hops >= 1:
                self.send((colour, phase, sub, direction, 1))

    def received(self, message):
        colour, phase, sub, direction, step = message
        plus, minus = reach(colour, phase, sub)
        if step < (plus if direction == 1 else minus):
            self.send((colour, phase, sub, direction, step + 1))
        if phase == 0:
            self.first[colour] += 1
            if self.first[colour] == SIZE[ORDERS[colour][0]] - 1:
                for k in subs_of(colour, 1):
                    self.begin(colour, 1, k)
                for k in subs_of(colour, 1):
                    self.begin(colour, 2, (0, k))
        elif phase == 1:
            offset = (-direction * step) % SIZE[ORDERS[colour][1]]
            self.begin(colour, 2, (offset, sub))
        self.count(message)


def plan(starts):
    free, heap = {}, []
    now = [0.0]

    def send(message):
        colour, phase, sub, direction, step = message
        size = 16384 if phase == 0 else 65536
        link = (ORDERS[colour][phase], direction)
        begin = max(now[0], free.get(link, 0.0))
        free[link] = begin + size / 46e3
        heapq.heappush(heap, (free[link] + 1.7, INDEX[message]))

    pending = []
    flow = Flow(send, pending.append)
    order = []
    for colour, start in enumerate(starts):
        heapq.heappush(heap, (start, -1 - colour))
    while heap or pending:
        if pending and not (heap and heap[0][0] <= now[0]):
            piece = pending.pop(0)
            order.append(piece)
            now[0] += 0.9 if piece[0] == 1 else 0.3
            continue
        arrival, which = heapq.heappop(heap)
        now[0] = max(now[0], arrival)
        order.append(which)
        if which < 0:
            flow.begin(-1 - which, 0, None)
        else:
            flow.received(MESSAGES[which])
    return order, now[0]


PLAN, MODEL_TIME = plan((3.0, 0.0, 1.5))


def kernel(
    tok, iq_hbm, ik_hbm, iv_hbm, oq_hbm, ok_hbm, ov_hbm, mq_hbm, mk_hbm, mv_hbm,
    proj, uq, uk, uv, nq, nk, nv,
    iq, ik, iv, oq, ok, ov, mq, mk, mv, in_sem,
    buf, tok2, ri, fr, pout, acc,
    rep_sem, ring_sem, tok_sem, fr_sem, out_sem, rep_send, ring_send, fr_send, out_send, tok_send, tok_local,
):
    r, f = lax.axis_index("replica"), lax.axis_index("fsdp")
    core, zh = r % 2, r // 2
    zl, x, y = f // 16, (f // 4) % 4, f % 4
    z = zh * 4 + zl
    at = {"x": x, "y": y, "z": z}

    def dev(xx, yy, zz):
        return {"replica": (zz // 4) * 2 + core, "fsdp": ((zz % 4) * 4 + xx) * 4 + yy}

    def neighbour(axis, direction):
        moved = dict(at)
        moved[axis] = (at[axis] + direction + SIZE[axis]) % SIZE[axis]
        return dev(moved["x"], moved["y"], moved["z"])

    peer_index = (zh * 2 + (1 - core), (1 - zh) * 2 + core, (1 - zh) * 2 + (1 - core))
    peers = tuple({"replica": p, "fsdp": f} for p in peer_index)
    neighbours = {(a, d): neighbour(a, d) for a in ("x", "y", "z") for d in (1, -1)}

    barrier = pltpu.get_barrier_semaphore()
    for target in peers + tuple(neighbours.values()):
        pl.semaphore_signal(barrier, inc=1, device_id=target, device_id_type=MESH)
    fetches = [
        pltpu.make_async_copy(src, dst, in_sem.at[i])
        for i, (src, dst) in enumerate(
            zip(
                (iq_hbm, ik_hbm, iv_hbm, oq_hbm, ok_hbm, ov_hbm, mq_hbm, mk_hbm, mv_hbm),
                (iq, ik, iv, oq, ok, ov, mq, mk, mv),
            )
        )
    ]
    for c in fetches:
        c.start()
    own_tokens = pltpu.make_async_copy(tok, tok2.at[0], tok_local)
    own_tokens.start()
    for c in fetches:
        c.wait()
    pl.semaphore_wait(barrier, 9)

    def remote(src, dst, send_sem, recv_sem, target):
        return pltpu.make_async_remote_copy(
            src_ref=src, dst_ref=dst, send_sem=send_sem, recv_sem=recv_sem, device_id=target, device_id_type=MESH
        )

    def col(index, width, extra=0):
        return pl.ds(pl.multiple_of(index * width + extra, 128), WIDTH if width == 512 else 128)

    def replica_copies(colour, d):
        p = peer_index[d]
        if colour < 2:
            pairs = ((iq.at[:, col(p, 512, colour * WIDTH)], ri.at[d, colour]),)
        else:
            pairs = (
                (ik.at[:, col(p, 128)], ri.at[d, 2, :, 0:128]),
                (iv.at[:, col(p, 128)], ri.at[d, 2, :, 128:256]),
            )
        return [
            remote(src, dst, rep_send.at[d, colour + i], rep_sem.at[d, colour + i], peers[d])
            for i, (src, dst) in enumerate(pairs)
        ]

    copies = {}
    for colour in (1, 2, 0):
        for d in (1, 2, 0):
            copies[colour, d] = replica_copies(colour, d)
            for c in copies[colour, d]:
                c.start()
    swap = remote(tok, tok2.at[1], tok_send, tok_sem, peers[0])
    swap.start()

    def update(colour):
        for d in range(3):
            for c in copies[colour, d]:
                c.wait_recv()
        if colour < 2:
            outer = oq[:, col(r, 512, colour * WIDTH)]
            inner = iq[:, col(r, 512, colour * WIDTH)]
            moment = mq[:, colour * WIDTH:(colour + 1) * WIDTH]
        else:
            outer = jnp.concatenate([ok[:, col(r, 128)], ov[:, col(r, 128)]], axis=1)
            inner = jnp.concatenate([ik[:, col(r, 128)], iv[:, col(r, 128)]], axis=1)
            moment = jnp.concatenate([mk[...], mv[...]], axis=1)
        total = outer - inner.astype(jnp.float32)
        for d in range(3):
            total += outer - ri[d, colour].astype(jnp.float32)
        pseudo = total * 0.25
        new_moment = MOMENTUM_BETA * moment + pseudo
        new_outer = outer - LEARN_RATE * (pseudo + MOMENTUM_BETA * new_moment)
        buf[colour, z, x, y] = new_outer.astype(jnp.bfloat16)
        if colour < 2:
            nq[:, colour * WIDTH:(colour + 1) * WIDTH] = new_moment
        else:
            nk[...] = new_moment[:, :128]
            nv[...] = new_moment[:, 128:]

    def block(colour, phase, sub, offset):
        axis = ORDERS[colour][phase]
        pos = dict(at)
        if phase == 2:
            second = ORDERS[colour][1]
            pos[second] = (at[second] + sub[0]) % SIZE[second]
            sub = sub[1]
        pos[axis] = (at[axis] + offset + SIZE[axis]) % SIZE[axis]
        if phase == 0:
            return buf.at[colour, pos["z"], pos["x"], pos["y"]]
        if colour == 0:
            return buf.at[0, pos["z"], :, pos["y"]]
        return buf.at[colour, pl.ds(sub * 4, 4), pos["x"], pos["y"]]

    def ring_copy(message):
        colour, phase, sub, direction, step = message
        src = block(colour, phase, sub, -direction * (step - 1))
        return remote(src, src, ring_send, ring_sem.at[INDEX[message]], neighbours[ORDERS[colour][phase], direction])

    def wait_ring(message):
        colour, phase, sub, direction, step = message
        dst = block(colour, phase, sub, -direction * step)
        remote(dst, dst, ring_send, ring_sem.at[INDEX[message]], neighbours[ORDERS[colour][phase], direction]).wait_recv()

    out_copies = []

    def send_out(i):
        colour, h = i // 2, i % 2
        rr = 2 * h + core
        if colour < 2:
            pairs = ((pout.at[i], proj.at[:, col(rr, 512, colour * WIDTH)]),)
        else:
            pairs = (
                (pout.at[i, :, 0:128], proj.at[:, col(rr, 128, 2048)]),
                (pout.at[i, :, 128:256], proj.at[:, col(rr, 128, 2560)]),
            )
        for j, (src, dst) in enumerate(pairs):
            c = remote(src, dst, out_send.at[i, j], out_sem.at[i, j], peers[0])
            c.start()
            out_copies.append(c)

    def finish(i, total):
        colour, h = i // 2, i % 2
        rr = 2 * h + core
        done = total.astype(jnp.bfloat16)
        pout[i] = done[256:]
        if colour < 2:
            proj[:, col(rr, 512, colour * WIDTH)] = done[:256]
        else:
            proj[:, col(rr, 128, 2048)] = done[:256, :128]
            proj[:, col(rr, 128, 2560)] = done[:256, 128:]
        send_out(i)

    def product(a, w):
        return jnp.dot(a, w, preferred_element_type=jnp.float32)

    done_pieces = []

    def multiply(piece):
        if not done_pieces:
            own_tokens.wait()
            swap.wait()
        done_pieces.append(piece)
        if piece[0] == 0:
            plane = (z + piece[1]) % 8
            columns = pl.ds(pl.multiple_of((plane % 4) * 512, 512), 512)
            part = product(tok2[:, :, columns].reshape(512, 512), buf[0, plane].reshape(512, WIDTH))
            acc[plane // 4] += part
            if sum(p[0] == 0 for p in done_pieces) == 8:
                finish(0, acc[0])
                finish(1, acc[1])
        elif piece[0] == 1:
            k = piece[1]
            w = buf[1, k * 4:(k + 1) * 4].reshape(2048, WIDTH)
            finish(2 + k, product(tok2[...].reshape(512, 2048), w))
        else:
            _, d, k = piece
            xx = (x + d) % 4
            a = jnp.concatenate(
                [tok2[:, :, pl.ds(pl.multiple_of(q * 512 + xx * 128, 128), 128)] for q in range(4)], axis=2
            )
            part = product(a.reshape(512, 512), buf[2, k * 4:(k + 1) * 4, xx].reshape(512, WIDTH))
            n = sum(p[0] == 2 and p[2] == k for p in done_pieces)
            if n == 1:
                acc[4 + k] = part
            elif n < 4:
                acc[4 + k] += part
            else:
                finish(4 + k, acc[4 + k] + part)

    acc[0:2] = jnp.zeros((2, 512, WIDTH), jnp.float32)
    flow = Flow(lambda message: ring_copy(message).start(), lambda piece: None)
    partner_copies = []
    for which in PLAN:
        if isinstance(which, tuple):
            multiply(which)
        elif which < 0:
            colour = -1 - which
            update(colour)
            flow.begin(colour, 0, None)
            c = remote(buf.at[colour, z, x, y], fr.at[0, colour], fr_send.at[0, colour], fr_sem.at[0, colour], peers[0])
            c.start()
            partner_copies.append(c)
        else:
            wait_ring(MESSAGES[which])
            flow.received(MESSAGES[which])

    z4 = (z + 4) % 8
    for colour in range(3):
        c = remote(buf.at[colour, z4, x, y], fr.at[1, colour], fr_send.at[1, colour], fr_sem.at[1, colour], peers[0])
        c.start()
        partner_copies.append(c)

    for c in partner_copies:
        c.wait()
    for source, owner in (
        (lambda c: buf[c, z, x, y], r),
        (lambda c: buf[c, z4, x, y], peer_index[1]),
        (lambda c: fr[0, c], peer_index[0]),
        (lambda c: fr[1, c], peer_index[2]),
    ):
        for colour in range(2):
            uq[:, col(owner, 512, colour * WIDTH)] = source(colour).astype(jnp.float32)
        both = source(2).astype(jnp.float32)
        uk[:, col(owner, 128)] = both[:, :128]
        uv[:, col(owner, 128)] = both[:, 128:]

    for c in out_copies:
        c.wait()
    for colour in range(3):
        for d in range(3):
            for c in copies[colour, d]:
                c.wait_send()
    for colour in range(3):
        done = buf.at[colour].reshape(128, ROWS, WIDTH).at[pl.ds(0, 127)]
        pltpu.make_async_copy(done, done, ring_send).wait()


def write_kernel(*refs):
    sources, targets, sem = refs[:7], refs[7:14], refs[14]
    copies = [pltpu.make_async_copy(src, dst, sem.at[i]) for i, (src, dst) in enumerate(zip(sources, targets))]
    for c in copies:
        c.start()
    for c in copies:
        c.wait()


def write_out(results):
    return pl.pallas_call(
        write_kernel,
        out_shape=tuple(jax.ShapeDtypeStruct(a.shape, a.dtype) for a in results),
        in_specs=[pl.BlockSpec(memory_space=pltpu.VMEM)] * 7,
        out_specs=(pl.BlockSpec(memory_space=pltpu.HBM),) * 7,
        scratch_shapes=[pltpu.SemaphoreType.DMA((7,))],
        compiler_params=pltpu.CompilerParams(vmem_limit_bytes=16 * 1024 * 1024),
        name="write_results",
    )(*results)


def per_device(
    tokens, inner_q, inner_k, inner_v, outer_q, outer_k, outer_v, moment_q, moment_k, value_momentum
):
    f32, bf16 = jnp.float32, jnp.bfloat16
    vmem = pl.BlockSpec(memory_space=pltpu.VMEM)
    out = pl.pallas_call(
        kernel,
        out_shape=(
            jax.ShapeDtypeStruct((256, 3072), bf16),
            jax.ShapeDtypeStruct((ROWS, 2048), f32),
            jax.ShapeDtypeStruct((ROWS, 512), f32),
            jax.ShapeDtypeStruct((ROWS, 512), f32),
            jax.ShapeDtypeStruct((ROWS, 512), f32),
            jax.ShapeDtypeStruct((ROWS, 128), f32),
            jax.ShapeDtypeStruct((ROWS, 128), f32),
        ),
        in_specs=[pl.BlockSpec(memory_space=pltpu.HBM)] * 10,
        out_specs=(vmem,) * 7,
        scratch_shapes=[
            pltpu.VMEM((ROWS, 2048), bf16),
            pltpu.VMEM((ROWS, 512), bf16),
            pltpu.VMEM((ROWS, 512), bf16),
            pltpu.VMEM((ROWS, 2048), f32),
            pltpu.VMEM((ROWS, 512), f32),
            pltpu.VMEM((ROWS, 512), f32),
            pltpu.VMEM((ROWS, 512), f32),
            pltpu.VMEM((ROWS, 128), f32),
            pltpu.VMEM((ROWS, 128), f32),
            pltpu.SemaphoreType.DMA((9,)),
            pltpu.VMEM((3, NZ, NX, NY, ROWS, WIDTH), bf16),
            pltpu.VMEM((2, 256, 2048), bf16),
            pltpu.VMEM((3, 3, ROWS, WIDTH), bf16),
            pltpu.VMEM((2, 3, ROWS, WIDTH), bf16),
            pltpu.VMEM((6, 256, WIDTH), bf16),
            pltpu.VMEM((6, 512, WIDTH), f32),
            pltpu.SemaphoreType.DMA((3, 4)),
            pltpu.SemaphoreType.DMA((len(MESSAGES),)),
            pltpu.SemaphoreType.DMA,
            pltpu.SemaphoreType.DMA((2, 3)),
            pltpu.SemaphoreType.DMA((6, 2)),
            pltpu.SemaphoreType.DMA((3, 4)),
            pltpu.SemaphoreType.DMA,
            pltpu.SemaphoreType.DMA((2, 3)),
            pltpu.SemaphoreType.DMA((6, 2)),
            pltpu.SemaphoreType.DMA,
            pltpu.SemaphoreType.DMA,
        ],
        compiler_params=pltpu.CompilerParams(
            collective_id=0, has_side_effects=True, vmem_limit_bytes=32 * 1024 * 1024
        ),
        name="outer_step_gather_project",
    )(*(
        pltpu.with_memory_space_constraint(a, pltpu.HBM)
        for a in (
            tokens, inner_q[0], inner_k[0], inner_v[0], outer_q, outer_k, outer_v, moment_q, moment_k, value_momentum
        )
    ))
    return tuple(write_out(out))


def solution(mesh):
    placed = (
        P(("replica", "fsdp"), None),
        P("replica", "fsdp", None),
        P("replica", "fsdp", None),
        P("replica", "fsdp", None),
        P("fsdp", None),
        P("fsdp", None),
        P("fsdp", None),
        P("fsdp", "replica"),
        P("fsdp", "replica"),
        P("fsdp", "replica"),
    )
    return jax.shard_map(
        per_device,
        mesh=mesh,
        in_specs=placed,
        out_specs=(
            P(("replica", "fsdp"), None),
            P("fsdp", None),
            P("fsdp", None),
            P("fsdp", None),
            P("fsdp", "replica"),
            P("fsdp", "replica"),
            P("fsdp", "replica"),
        ),
        check_vma=False,
    )
```
